128 devices in a mesh: hours: 8 (over x_hi, z), sensor: 16 (over x_lo, y, core).
Axes of the slice: x: 4 (x_hi: 2, x_lo: 2; x = x_hi * 2 + x_lo), y: 4, z: 4, core: 2. Of those that a mesh axis runs over, the one named last changes fastest.
Arguments:
- coefficients: float32 [577, 16, 512], P(None, 'sensor'), may hold values from 5e-05 to 0.0053
- sky: float32 [577, 32768], P(None, ('hours', 'sensor')), may hold values from 0.1 to 10
- outdoor_air_warmth: float32 [32768], replicated, may hold values from -5 to 40
- hour_column: int32 [32768], replicated, may hold values from 0 to 32767, as said below
- module_of: int32 [16, 8, 64], P('sensor', 'hours'), may hold values from 0 to 7, as said below
Outputs:
- power: float32 [16, 8, 64, 32768], P('sensor', 'hours')
The draws below stay inside these ranges and needn't reach their ends.
Inputs may be any that keep to these rules, and one draw needn't show every extreme that they name: `hour_column`: every column appears once, and the column of a time step lies in the same aligned run of 256 columns as the step itself. `module_of`: each module of a tracker row holds exactly 8 of the row's points.
All inputs are finite; a program needn't handle non-finite values.
Results may differ from the reference program's by a relative error of at most 0.0003.
Values sent between devices are 32-bit elements; how exact they have to be, the bound alone decides.
A program may use at most 128 MiB of HBM per device.

```python
import math
import jax
import jax.numpy as jnp
from jax import lax

PATCHES = 577
BLOCK_ROWS = 8
POINTS = 64
MODS = 8
WINDOW = 128
STEP_DEV = 256
BLOCKS = 16
BLOCK_SENS = 512
STEPS = 32768


def draw_coefficients(key, part):
    scale_key, entry_key = jax.random.split(jax.random.fold_in(key, 11))
    scales = jnp.exp(jax.random.uniform(scale_key, (1, BLOCKS, BLOCK_SENS), jnp.float32, math.log(0.15), math.log(1.5)))
    entries = jnp.exp(jax.random.uniform(entry_key, (PATCHES, BLOCKS, BLOCK_SENS), jnp.float32, math.log(0.00035), math.log(0.0035)))
    return (scales * entries).astype(jnp.float32)


def draw_hour_column(key, part):
    run_count = STEPS // STEP_DEV
    run_keys = jax.random.split(jax.random.fold_in(key, 37), run_count)
    orders = jax.vmap(lambda run_key: jax.random.permutation(run_key, STEP_DEV))(run_keys)
    starts = (jnp.arange(run_count, dtype=jnp.int32) * STEP_DEV)[:, None]
    return (orders.astype(jnp.int32) + starts).reshape(STEPS).astype(jnp.int32)


def draw_module_of(key, part):
    row_keys = jax.random.split(jax.random.fold_in(key, 23), BLOCKS * BLOCK_ROWS)
    orders = jax.vmap(lambda row_key: jax.random.permutation(row_key, POINTS))(row_keys)
    return (orders % MODS).astype(jnp.int32).reshape(BLOCKS, BLOCK_ROWS, POINTS)


def block_scale(key, dims, cuts, least, high):
    level, own = 1.0, jax.random.fold_in(key, 6)
    for axis_at, shards_of in cuts:
        steps = jnp.exp(jax.random.uniform(jax.random.fold_in(own, axis_at), (shards_of,), jnp.float32, least / len(cuts), high / len(cuts)))
        level = level * jnp.repeat(steps, dims[axis_at] // shards_of).reshape([-1 if axis == axis_at else 1 for axis in range(len(dims))])
    return level


def setup_inputs(seed: int = 0) -> dict:
    streams_of = jax.random.split(jax.random.key(seed), 6)
    coefficients = draw_coefficients(jax.random.fold_in(streams_of[5], 71), 0)
    sky = jnp.clip(jnp.exp(math.log(10.0) - 4.6051702 * jax.random.uniform(streams_of[1], (PATCHES, STEPS), jnp.float32) ** block_scale(streams_of[1], (PATCHES, STEPS), ((1, 128),), -0.2, 0.2)), 0.1, 10.0)
    outdoor_air_warmth = jnp.clip(jax.random.uniform(streams_of[2], (STEPS,), jnp.float32, -5.0, 40.0), -5.0, 40.0)
    hour_column = draw_hour_column(jax.random.fold_in(streams_of[5], 71), 0)
    module_of = draw_module_of(jax.random.fold_in(streams_of[5], 71), 0)
    return dict(coefficients=coefficients, sky=sky, outdoor_air_warmth=outdoor_air_warmth, hour_column=hour_column, module_of=module_of)


loss_multiplier = 0.0045
panel_warmup = 50.0
nominal_test_warmth = 25.0


def thermal_power(incident_flux, modules, outdoor_air_warmth):
    onehot = (modules[:, :, None] == jnp.arange(MODS, dtype=jnp.int32)[None, None, :]).astype(jnp.float32)
    module_average = jnp.einsum("rqm,rqt->rmt", onehot, incident_flux, precision=lax.Precision.HIGHEST) / (POINTS // MODS)
    heat = lax.reduce_window(module_average, jnp.float32(0.0), lax.add, (1, 1, WINDOW), (1, 1, 1), ((0, 0), (0, 0), (WINDOW - 1, 0))) / WINDOW
    smoothing_span = jnp.einsum("rqm,rmt->rqt", onehot, heat, precision=lax.Precision.HIGHEST)
    junction_warmth = outdoor_air_warmth[None, None, :] + panel_warmup * smoothing_span
    return incident_flux * (1.0 - loss_multiplier * (junction_warmth - nominal_test_warmth))


def reference(coefficients, sky, outdoor_air_warmth, hour_column, module_of):
    def one_block(items):
        block_coeff, block_modules = items
        stored = lax.dot_general(block_coeff, sky, (((0,), (0,)), ((), ())), precision=lax.Precision.HIGHEST, preferred_element_type=jnp.float32)
        incident_flux = jnp.take(stored, hour_column, axis=1).reshape(BLOCK_ROWS, POINTS, STEPS)
        return thermal_power(incident_flux, block_modules, outdoor_air_warmth)

    return lax.map(one_block, (jnp.moveaxis(coefficients, 1, 0), module_of))
```

```python
import functools

import jax
import jax.numpy as jnp
from jax import lax
from jax.experimental import pallas as pl
from jax.experimental.pallas import tpu as pltpu
from jax.sharding import PartitionSpec as P

MESH = pl.DeviceIdType.MESH
PATCHES = 577
ROWS = 584
DEPTH = 640
POINTS = 64
MODS = 8
WINDOW = 128
STEPS = 32768
WINDOWS = STEPS // WINDOW
SLOTS = 16

X, Y, Z = 0, 1, 2
PLANS = ((X, Y, Z, 480), (Z, Y, X, 416))

LOSS = 0.0045
WARMUP = 50.0
NOMINAL = 25.0


def coordinates():
    h, s = lax.axis_index("hours"), lax.axis_index("sensor")
    return (h // 4) * 2 + s // 8, (s // 2) % 4, h % 4, s % 2


def shifted(place, axis, by):
    moved = list(place)
    moved[axis] = (moved[axis] + by) % 4
    return tuple(moved)


def sibling(place):
    return place[0], place[1], place[2], 1 - place[3]


def device(place):
    x, y, z, c = place
    return (x // 2) * 4 + z, ((x % 2) * 4 + y) * 2 + c


def slot_of(i, j):
    return i * 4 + j


def middle(start, stop):
    return start + (stop - start) // 16 * 8


ORDER = (
    (3, 0), (1, 0), (0, 3), (0, 1), (2, 0), (0, 2), (3, 3), (1, 1), (3, 1), (1, 3),
    (2, 3), (2, 1), (3, 2), (1, 2), (2, 2),
)


def two_parts(value):
    high = value.astype(jnp.bfloat16)
    return high, (value - high.astype(jnp.float32)).astype(jnp.bfloat16)


def gather_kernel(
    coef_hbm, sky_hbm, hour_hbm, out_ref,
    coef_raw, sky_raw, hour_raw, coef_own, coef_sib, coef_x, coef_high, coef_low, sky_buf, sky_high, sky_low, prod,
    load_sem, sky_sems, sky_send, coef_sems, coef_send, prod_send, prod_recv,
):
    place = coordinates()
    x, y, z, c = place
    h, s = device(place)
    me = h * 16 + s
    loads = [
        pltpu.make_async_copy(sky_hbm, sky_raw, load_sem.at[0]),
        pltpu.make_async_copy(hour_hbm.at[pl.ds(pl.multiple_of((me // 4) * 8, 8), 8)], hour_raw, load_sem.at[1]),
        pltpu.make_async_copy(coef_hbm, coef_raw, load_sem.at[2]),
    ]
    for load in loads:
        load.start()

    partners = [sibling(place), shifted(place, Y, 1), shifted(place, Y, 3)]
    for axis in (X, Z):
        for k in (1, 2, 3):
            partners += [shifted(place, axis, k), sibling(shifted(place, axis, k))]
    barrier = pltpu.get_barrier_semaphore()
    for partner in partners:
        pl.semaphore_signal(barrier, inc=1, device_id=device(partner), device_id_type=MESH)

    loads[0].wait()
    loads[1].wait()
    sky_parts = two_parts(sky_raw[...])
    for half in range(2):
        column = hour_raw[pl.ds((me % 4) * 2 + half, 1), :] - me * 256
        chosen = (lax.broadcasted_iota(jnp.int32, (256, 128), 0) == column).astype(jnp.bfloat16)
        ordered = sum(jnp.dot(part, chosen, preferred_element_type=jnp.float32) for part in sky_parts)
        sky_buf[half, 0, pl.ds(PATCHES - 1, 8), :] = jnp.zeros((8, 128), jnp.float32)
        sky_buf[half, 0, pl.ds(0, PATCHES), :] = ordered
    sky_high[pl.ds(576, 64), :] = jnp.zeros((64, 128), jnp.bfloat16)
    sky_low[pl.ds(576, 64), :] = jnp.zeros((64, 128), jnp.bfloat16)
    pl.semaphore_wait(barrier, len(partners))

    def rows_of(half, part):
        cut = PLANS[half][3]
        return (0, cut) if part == 0 else (cut, ROWS)

    def send_sky(half, part, i, j, axis, by, which=None):
        start, stop = rows_of(half, part)
        if which == 0:
            stop = middle(start, stop)
        elif which == 1:
            start = middle(start, stop)
        first, second = PLANS[half][0], PLANS[half][1]
        to = slot_of((i - by) % 4, j) if axis == first else slot_of(i, (j - by) % 4)
        rows = pl.ds(start, stop - start)
        pltpu.make_async_remote_copy(
            src_ref=sky_buf.at[half, slot_of(i, j), rows],
            dst_ref=sky_buf.at[half, to, rows],
            send_sem=sky_send.at[half],
            recv_sem=sky_sems.at[half, part, to, which or 0],
            device_id=device(shifted(place, axis, by)),
            device_id_type=MESH,
        ).start()

    def await_sky(half, part, i, j):
        first, second = PLANS[half][:2] if part == 0 else PLANS[half][1::-1]
        along, across = (i, j) if part == 0 else (j, i)
        start, stop = rows_of(half, part)
        slot = slot_of(i, j)

        def wait(which, start, stop):
            rows = sky_buf.at[half, slot, pl.ds(start, stop - start)]
            pltpu.make_async_copy(rows, rows, sky_sems.at[half, part, slot, which]).wait()

        if across == 2 or (across == 0 and along == 2):
            wait(0, start, middle(start, stop))
            wait(1, middle(start, stop), stop)
        else:
            wait(0, start, stop)
        if across == 0:
            send_sky(half, part, i, j, second, 1)
            send_sky(half, part, i, j, second, -1)
            if along == 3:
                send_sky(half, part, i, j, first, 1, 0)
            if along == 1:
                send_sky(half, part, i, j, first, -1, 1)
        if across == 3:
            send_sky(half, part, i, j, second, 1, 0)
        if across == 1:
            send_sky(half, part, i, j, second, -1, 1)

    for half in range(2):
        for part in range(2):
            for axis in PLANS[half][:2]:
                send_sky(half, part, 0, 0, axis, 1)
                send_sky(half, part, 0, 0, axis, -1)

    loads[2].wait()
    coef_own[:, pl.ds(512, 128)] = jnp.zeros((512, 128), jnp.float32)
    for tile in range(4):
        lanes = pl.ds(tile * 128, 128)
        whole = coef_raw[:, 0, lanes]
        coef_own[lanes, pl.ds(0, PATCHES)] = whole.T

    def coef_copy(src, dst, sem, to):
        return pltpu.make_async_remote_copy(
            src_ref=src, dst_ref=dst, send_sem=coef_send.at[sem], recv_sem=coef_sems.at[sem],
            device_id=device(to), device_id_type=MESH,
        )

    own_row = coef_own.at[pl.ds(pl.multiple_of(h * 64, 64), 64)]
    to_next = coef_copy(own_row, coef_x.at[1, 0], 1, shifted(place, X, 1))
    to_last = coef_copy(own_row, coef_x.at[0, 0], 2, shifted(place, X, 3))
    to_sibling = coef_copy(coef_own, coef_sib, 0, sibling(place))
    to_next.start()
    to_last.start()
    to_sibling.start()

    def put_coef(half, k, other, value):
        high, low = two_parts(value)
        rows = pl.ds((k * 2 + other) * 64, 64)
        coef_high[half, rows, :] = high
        coef_low[half, rows, :] = low

    def row_at(half, k):
        at = (x // 2) * 4 + (z + k) % 4 if half == 0 else (((x + k) % 4) // 2) * 4 + z
        return pl.ds(pl.multiple_of(at * 64, 64), 64)

    for k in range(4):
        put_coef(0, k, 0, coef_own[row_at(0, k), :])
    for k in (0, 2):
        put_coef(1, k, 0, coef_own[row_at(1, k), :])
    to_sibling.wait()
    for k in range(4):
        put_coef(0, k, 1, coef_sib[row_at(0, k), :])
    for k in (0, 2):
        put_coef(1, k, 1, coef_sib[row_at(1, k), :])

    def multiply(half, i, j):
        slot = slot_of(i, j)
        axis = PLANS[half][2]
        high, low = two_parts(sky_buf[half, slot, pl.ds(0, 576), :])
        sky_high[pl.ds(0, 576), :] = high
        sky_low[pl.ds(0, 576), :] = low
        high, low = two_parts(sky_buf[half, slot, pl.ds(576, 8), :])
        pad = jnp.zeros((8, 128), jnp.bfloat16)
        sky_high[pl.ds(576, 16), :] = jnp.concatenate([high, pad], axis=0)
        sky_low[pl.ds(576, 16), :] = jnp.concatenate([low, pad], axis=0)

        @pl.loop(0, 2)
        def _(tile):
            rows = pl.ds(pl.multiple_of(tile * 256, 256), 256)
            prod[half, slot, rows, :] = (
                jnp.dot(coef_high[half, rows, :], sky_low[...], preferred_element_type=jnp.float32)
                + jnp.dot(coef_low[half, rows, :], sky_high[...], preferred_element_type=jnp.float32)
            ) + jnp.dot(coef_high[half, rows, :], sky_high[...], preferred_element_type=jnp.float32)

        oh, os = device(shifted(shifted(place, PLANS[half][0], i), PLANS[half][1], j))
        window = (oh * 16 + os) * 2 + half
        out_ref[window] = prod[half, slot, pl.ds(0, 64), :]
        for k in (2, 1, 3, 0):
            for other in range(2):
                if (k, other) == (0, 0):
                    continue
                to = shifted(place, axis, k)
                pltpu.make_async_remote_copy(
                    src_ref=prod.at[half, slot, pl.ds((k * 2 + other) * 64, 64)],
                    dst_ref=out_ref.at[window],
                    send_sem=prod_send.at[half],
                    recv_sem=prod_recv,
                    device_id=device(sibling(to) if other else to),
                    device_id_type=MESH,
                ).start()

    multiply(0, 0, 0)
    to_next.wait()
    to_last.wait()
    on = [coef_copy(coef_x.at[n, 0], coef_x.at[n, 1], 3 + n, sibling(place)) for n in range(2)]
    for copy in on:
        copy.start()
    for half in range(2):
        for i, j in ORDER[:4]:
            await_sky(half, 0, i, j)
            await_sky(half, 1, i, j)
    for n, k in enumerate((1, 3)):
        put_coef(1, k, 0, coef_x[n, 0])
    for n, k in enumerate((1, 3)):
        on[n].wait()
        put_coef(1, k, 1, coef_x[n, 1])
    multiply(1, 0, 0)
    for n, (i, j) in enumerate(ORDER):
        for half in range(2):
            if n >= 4:
                await_sky(half, 0, i, j)
                await_sky(half, 1, i, j)
            multiply(half, i, j)

    for half in range(2):
        sent = sky_buf.at[half, pl.ds(0, 15)]
        pltpu.make_async_copy(sent, sent, sky_send.at[half]).wait()
        sent = prod.at[half, pl.ds(0, 14)]
        pltpu.make_async_copy(sent, sent, prod_send.at[half]).wait()
    came = out_ref.at[pl.ds(0, WINDOWS // 8 * 7)]
    pltpu.make_async_copy(came, came, prod_recv).wait()


def irradiance(coefficients, sky, hours):
    f32, bf16 = jnp.float32, jnp.bfloat16
    vmem, dma = pltpu.VMEM, pltpu.SemaphoreType.DMA
    return pl.pallas_call(
        gather_kernel,
        out_shape=jax.ShapeDtypeStruct((WINDOWS, POINTS, WINDOW), f32),
        in_specs=[pl.BlockSpec(memory_space=pl.ANY)] * 3,
        out_specs=pl.BlockSpec(memory_space=pltpu.VMEM),
        scratch_shapes=[
            vmem((PATCHES, 1, 512), f32),
            vmem((PATCHES, 256), f32),
            vmem((8, 128), jnp.int32),
            vmem((512, DEPTH), f32),
            vmem((512, DEPTH), f32),
            vmem((2, 2, 64, DEPTH), f32),
            vmem((2, 512, DEPTH), bf16),
            vmem((2, 512, DEPTH), bf16),
            vmem((2, SLOTS, ROWS, 128), f32),
            vmem((DEPTH, 128), bf16),
            vmem((DEPTH, 128), bf16),
            vmem((2, SLOTS, 512, 128), f32),
            dma((3,)),
            dma((2, 2, SLOTS, 2)),
            dma((2,)),
            dma((5,)),
            dma((5,)),
            dma((2,)),
            dma,
        ],
        compiler_params=pltpu.CompilerParams(
            collective_id=0, has_side_effects=True, vmem_limit_bytes=56 << 20
        ),
        name="irradiance",
    )(coefficients, sky, hours)


GROUP = 16


def thermal_kernel(flux_ref, air_ref, module_ref, out_ref, means, factor):
    f32, bf16 = jnp.float32, jnp.bfloat16

    @pl.when(pl.program_id(0) == 0)
    def _():
        means[pl.ds(0, MODS), :] = jnp.zeros((MODS, WINDOW), f32)

    @pl.when(pl.program_id(0) > 0)
    def _():
        means[pl.ds(0, MODS), :] = means[pl.ds(GROUP * MODS, MODS), :]

    member = lax.broadcasted_iota(jnp.int32, (MODS, POINTS), 0) == module_ref[...]
    onehot = member.astype(bf16)
    both = jnp.concatenate([onehot, onehot], axis=1)
    for w in range(GROUP):
        stacked = jnp.concatenate(two_parts(flux_ref[w]), axis=0)
        mean = jnp.dot(both, stacked, preferred_element_type=f32) / (POINTS // MODS)
        means[pl.ds((w + 1) * MODS, MODS), :] = mean
    row = lax.broadcasted_iota(jnp.int32, (WINDOW, WINDOW), 0)
    col = lax.broadcasted_iota(jnp.int32, (WINDOW, WINDOW), 1)
    upper, lower = (row <= col).astype(bf16), (row > col).astype(bf16)
    heat = jnp.zeros((GROUP * MODS, WINDOW), f32)
    for first, weights in ((MODS, upper), (0, lower)):
        for part in two_parts(means[pl.ds(first, GROUP * MODS), :]):
            heat = heat + jnp.dot(part, weights, preferred_element_type=f32)
    heat = heat / WINDOW
    name = lax.broadcasted_iota(jnp.int32, (MODS, WINDOW), 0).astype(bf16)
    index = lax.dot_general(onehot, name, (((0,), (0,)), ((), ())), preferred_element_type=f32)
    index = index.astype(jnp.int32)
    for w in range(GROUP):
        warmth = air_ref[pl.ds(w, 1), :] + WARMUP * heat[w * MODS : (w + 1) * MODS, :]
        scale = 1.0 - LOSS * (warmth - NOMINAL)
        for r in range(POINTS // 8):
            spread = jnp.take_along_axis(scale, index[r * 8 : (r + 1) * 8, :], axis=0)
            rows = pl.ds(r * 8, 8)
            out_ref[rows, pl.ds(w * WINDOW, WINDOW)] = flux_ref[w, rows, :] * spread


def thermal_power(flux, air, modules):
    return pl.pallas_call(
        thermal_kernel,
        grid=(WINDOWS // GROUP,),
        out_shape=jax.ShapeDtypeStruct((POINTS, STEPS), jnp.float32),
        in_specs=[
            pl.BlockSpec((GROUP, POINTS, WINDOW), lambda g: (g, 0, 0)),
            pl.BlockSpec((GROUP, WINDOW), lambda g: (g, 0)),
            pl.BlockSpec((1, POINTS), lambda g: (0, 0)),
        ],
        out_specs=pl.BlockSpec((POINTS, GROUP * WINDOW), lambda g: (0, g)),
        scratch_shapes=[
            pltpu.VMEM(((GROUP + 1) * MODS, WINDOW), jnp.float32),
            pltpu.VMEM((8, WINDOW), jnp.float32),
        ],
        name="thermal",
    )(flux, air, modules)


def shards(coefficients, sky, outdoor_air_warmth, hour_column, module_of):
    flux = irradiance(coefficients, sky, hour_column.reshape(WINDOWS, WINDOW))
    power = thermal_power(flux, outdoor_air_warmth.reshape(WINDOWS, WINDOW), module_of.reshape(1, POINTS))
    return power.reshape(1, 1, POINTS, STEPS)


def solution(mesh):
    return jax.shard_map(
        shards,
        mesh=mesh,
        in_specs=(
            P(None, "sensor", None),
            P(None, ("hours", "sensor")),
            P(),
            P(),
            P("sensor", "hours", None),
        ),
        out_specs=P("sensor", "hours", None, None),
        check_vma=False,
    )
```

```python
import functools

import jax
import jax.numpy as jnp
from jax import lax
from jax.experimental import pallas as pl
from jax.experimental.pallas import tpu as pltpu
from jax.sharding import PartitionSpec as P

MESH = pl.DeviceIdType.MESH
PATCHES = 577
ROWS = 584
DEPTH = 640
POINTS = 64
MODS = 8
WINDOW = 128
STEPS = 32768
WINDOWS = STEPS // WINDOW
SLOTS = 16

CUT = 408
VLIM = 32 << 20

LOSS = 0.0045
WARMUP = 50.0
NOMINAL = 25.0


def coordinates():
    h, s = lax.axis_index("hours"), lax.axis_index("sensor")
    return (h // 4) * 2 + s // 8, (s // 2) % 4, h % 4, s % 2


def along_first(place, by):
    x, y, z, c = place
    return (x + by * (1 - c)) % 4, y, (z + by * c) % 4, c


def along_second(place, by):
    x, y, z, c = place
    return x, (y + by) % 4, z, c


def along_third(place, by):
    x, y, z, c = place
    return (x + by * c) % 4, y, (z + by * (1 - c)) % 4, c


def along_x(place, by):
    x, y, z, c = place
    return (x + by) % 4, y, z, c


def sibling(place):
    x, y, z, c = place
    return x, y, z, 1 - c


def device(place):
    x, y, z, c = place
    return (x // 2) * 4 + z, ((x % 2) * 4 + y) * 2 + c


def slot_of(i, j):
    return i * 4 + j


def middle(start, stop):
    return start + (stop - start) // 16 * 8


def two_parts(value):
    high = value.astype(jnp.bfloat16)
    return high, (value - high.astype(jnp.float32)).astype(jnp.bfloat16)


def gather_kernel(
    coef_hbm, sky_hbm, hour_hbm, out_ref,
    coef_raw, sky_raw, hour_raw, coef_own, coef_sib, coef_x, coef_high, coef_low, sky_buf, sky_high, sky_low, prod,
    load_sem, sky_sems, sky_send, coef_sems, coef_send, prod_send, prod_recv, prod_own,
):
    place = coordinates()
    x, y, z, c = place
    h, s = device(place)
    me = h * 16 + s
    loads = [
        pltpu.make_async_copy(sky_hbm, sky_raw, load_sem.at[0]),
        pltpu.make_async_copy(hour_hbm.at[pl.ds(pl.multiple_of((me // 4) * 8, 8), 8)], hour_raw, load_sem.at[1]),
        pltpu.make_async_copy(coef_hbm, coef_raw, load_sem.at[2]),
    ]
    for load in loads:
        load.start()

    partners = [along_second(place, 1), along_second(place, 3), sibling(place)]
    for k in (1, 2, 3):
        for partner in (along_third(place, k), along_first(place, k)):
            partners += [partner, sibling(partner)]
    barrier = pltpu.get_barrier_semaphore()
    for partner in partners:
        pl.semaphore_signal(barrier, inc=1, device_id=device(partner), device_id_type=MESH)

    loads[0].wait()
    loads[1].wait()
    sky_parts = two_parts(sky_raw[...])
    sky_buf[0, pl.ds(PATCHES - 1, 8), :] = jnp.zeros((8, 256), jnp.float32)
    for half in range(2):
        column = hour_raw[pl.ds((me % 4) * 2 + half, 1), :] - me * 256
        chosen = (lax.broadcasted_iota(jnp.int32, (256, 128), 0) == column).astype(jnp.bfloat16)
        ordered = sum(jnp.dot(part, chosen, preferred_element_type=jnp.float32) for part in sky_parts)
        sky_buf[0, pl.ds(0, PATCHES), pl.ds(half * 128, 128)] = ordered
    sky_high[pl.ds(576, 64), :] = jnp.zeros((64, 256), jnp.bfloat16)
    sky_low[pl.ds(576, 64), :] = jnp.zeros((64, 256), jnp.bfloat16)
    pl.semaphore_wait(barrier, len(partners))

    rows_of = ((0, CUT), (CUT, ROWS))

    def send_sky(part, i, j, second, by, which=None):
        start, stop = rows_of[part]
        if which == 0:
            stop = middle(start, stop)
        elif which == 1:
            start = middle(start, stop)
        to = slot_of(i, (j - by) % 4) if second else slot_of((i - by) % 4, j)
        rows = pl.ds(start, stop - start)
        pltpu.make_async_remote_copy(
            src_ref=sky_buf.at[slot_of(i, j), rows],
            dst_ref=sky_buf.at[to, rows],
            send_sem=sky_send,
            recv_sem=sky_sems.at[part, to, which or 0],
            device_id=device((along_second if second else along_first)(place, by % 4)),
            device_id_type=MESH,
        ).start()

    def await_sky(part, i, j):
        along, across = (i, j) if part == 0 else (j, i)
        start, stop = rows_of[part]
        slot = slot_of(i, j)

        def wait(which, start, stop):
            rows = sky_buf.at[slot, pl.ds(start, stop - start)]
            pltpu.make_async_copy(rows, rows, sky_sems.at[part, slot, which]).wait()

        if across == 2 or (across == 0 and along == 2):
            wait(0, start, middle(start, stop))
            wait(1, middle(start, stop), stop)
        elif (part, i) == (0, 0):
            wait(0, start, middle(start, stop))
            wait(1, middle(start, stop), stop)
        else:
            wait(0, start, stop)
        inner, outer = part == 1, part == 0
        if across == 0:
            if along == 3:
                send_sky(part, i, j, inner, 1, 0)
            if along == 1:
                send_sky(part, i, j, inner, -1, 1)
            send_sky(part, i, j, outer, 1)
            send_sky(part, i, j, outer, -1)
        if across == 3:
            send_sky(part, i, j, outer, 1, 0)
        if across == 1:
            send_sky(part, i, j, outer, -1, 1)

    for part, second, which in ((0, False, None), (1, True, None), (0, True, 0), (1, False, None)):
        send_sky(part, 0, 0, second, 1, which)
        send_sky(part, 0, 0, second, -1, which)

    loads[2].wait()
    coef_own[:, pl.ds(512, 128)] = jnp.zeros((512, 128), jnp.float32)
    for tile in range(4):
        lanes = pl.ds(tile * 128, 128)
        whole = coef_raw[:, 0, lanes]
        coef_own[lanes, pl.ds(0, PATCHES)] = whole.T

    def coef_copy(src, dst, sem, to):
        return pltpu.make_async_remote_copy(
            src_ref=src, dst_ref=dst, send_sem=coef_send.at[sem], recv_sem=coef_sems.at[sem],
            device_id=device(to), device_id_type=MESH,
        )

    def row_of(place):
        return pl.ds(pl.multiple_of(device(place)[0] * 64, 64), 64)

    def put_coef(k, other, value):
        high, low = two_parts(value)
        rows = pl.ds((k * 2 + other) * 64, 64)
        coef_high[rows, :] = high
        coef_low[rows, :] = low

    def x_copies(source, other):
        return [
            coef_copy(source.at[row_of(place)], coef_x.at[n, other], 1 + n * 2 + other, along_x(place, by))
            for n, by in ((0, 3), (1, 1))
        ]

    to_sibling = coef_copy(coef_own, coef_sib, 0, sibling(place))
    to_sibling.start()

    @pl.when(c == 1)
    def _():
        for copy in x_copies(coef_own, 0):
            copy.start()

    for k in (0, 2):
        put_coef(k, 0, coef_own[row_of(along_third(place, k)), :])

    @pl.when(c == 0)
    def _():
        for k in (1, 3):
            put_coef(k, 0, coef_own[row_of(along_third(place, k)), :])

    to_sibling.wait()

    @pl.when(c == 1)
    def _():
        for copy in x_copies(coef_sib, 1):
            copy.start()

    for k in (0, 2):
        put_coef(k, 1, coef_sib[row_of(along_third(place, k)), :])

    @pl.when(c == 0)
    def _():
        for k in (1, 3):
            put_coef(k, 1, coef_sib[row_of(along_third(place, k)), :])

    def await_all(*parts):
        for part, i, j in parts:
            await_sky(part, i, j)

    await_all((1, 0, 3), (1, 0, 1))
    send_sky(0, 0, 0, True, 1, 1)
    send_sky(0, 0, 0, True, -1, 1)
    await_all((0, 3, 0), (0, 1, 0), (1, 3, 0), (1, 1, 0))

    @pl.when(c == 1)
    def _():
        for other in range(2):
            for n, copy in enumerate(x_copies((coef_own, coef_sib)[other], other)):
                copy.wait()
                put_coef(2 * n + 1, other, coef_x[n, other])

    def multiply(i, j):
        slot = slot_of(i, j)
        high, low = two_parts(sky_buf[slot, pl.ds(0, 576), :])
        sky_high[pl.ds(0, 576), :] = high
        sky_low[pl.ds(0, 576), :] = low
        high, low = two_parts(sky_buf[slot, pl.ds(576, 8), :])
        pad = jnp.zeros((8, 256), jnp.bfloat16)
        sky_high[pl.ds(576, 16), :] = jnp.concatenate([high, pad], axis=0)
        sky_low[pl.ds(576, 16), :] = jnp.concatenate([low, pad], axis=0)

        @pl.loop(0, 2)
        def _(tile):
            rows = pl.ds(pl.multiple_of(tile * 256, 256), 256)
            both = (
                jnp.dot(coef_high[rows, :], sky_low[...], preferred_element_type=jnp.float32)
                + jnp.dot(coef_low[rows, :], sky_high[...], preferred_element_type=jnp.float32)
            ) + jnp.dot(coef_high[rows, :], sky_high[...], preferred_element_type=jnp.float32)
            for half in range(2):
                prod[slot, half, rows, :] = both[:, half * 128 : (half + 1) * 128]

        owner_h, owner_s = device(along_second(along_first(place, i), j))
        windows = pl.ds((owner_h * 16 + owner_s) * 2, 2)
        for k in (2, 1, 3, 0):
            for other in range(2):
                source = prod.at[slot, :, pl.ds((k * 2 + other) * 64, 64)]
                if (k, other) == (0, 0):
                    pltpu.make_async_copy(source, out_ref.at[windows], prod_own).start()
                    continue
                to = along_third(place, k)
                pltpu.make_async_remote_copy(
                    src_ref=source,
                    dst_ref=out_ref.at[windows],
                    send_sem=prod_send,
                    recv_sem=prod_recv,
                    device_id=device(sibling(to) if other else to),
                    device_id_type=MESH,
                ).start()

    def multiply_all(*chunks):
        for i, j in chunks:
            multiply(i, j)

    multiply_all((0, 0), (3, 0), (1, 0))
    await_all((1, 0, 2), (1, 3, 3), (1, 3, 1), (1, 1, 3), (1, 1, 1), (0, 2, 0), (1, 2, 0))
    multiply_all((2, 0))
    await_all((0, 0, 3), (0, 0, 1))
    multiply_all((0, 3), (0, 1))
    await_all((1, 3, 2), (1, 1, 2))
    await_all((0, 3, 3), (0, 3, 1))
    multiply_all((3, 3), (3, 1))
    await_all((0, 1, 3), (0, 1, 1))
    multiply_all((1, 3), (1, 1))
    await_all((1, 2, 3), (1, 2, 1), (1, 2, 2), (0, 2, 3), (0, 2, 1))
    multiply_all((2, 3), (2, 1))
    for i in (0, 3, 1, 2):
        await_all((0, i, 2))
        multiply_all((i, 2))

    def finish(ref, sem):
        pltpu.make_async_copy(ref, ref, sem).wait()

    finish(sky_buf.at[pl.ds(0, 15)], sky_send)
    finish(prod.at[pl.ds(0, 14)], prod_send)
    finish(prod.at[pl.ds(0, 2)], prod_own)
    finish(out_ref.at[pl.ds(0, WINDOWS // 8 * 7)], prod_recv)

def irradiance(coefficients, sky, hours):
    coefficients, sky, hours = [pltpu.with_memory_space_constraint(a, pltpu.HBM) for a in (coefficients, sky, hours)]
    f32, bf16 = jnp.float32, jnp.bfloat16
    vmem, dma = pltpu.VMEM, pltpu.SemaphoreType.DMA
    return pl.pallas_call(
        gather_kernel,
        out_shape=jax.ShapeDtypeStruct((WINDOWS, POINTS, WINDOW), f32),
        in_specs=[pl.BlockSpec(memory_space=pltpu.HBM)] * 3,
        out_specs=pl.BlockSpec(memory_space=pl.ANY),
        scratch_shapes=[
            vmem((PATCHES, 1, 512), f32),
            vmem((PATCHES, 256), f32),
            vmem((8, 128), jnp.int32),
            vmem((512, DEPTH), f32),
            vmem((512, DEPTH), f32),
            vmem((2, 2, 64, DEPTH), f32),
            vmem((512, DEPTH), bf16),
            vmem((512, DEPTH), bf16),
            vmem((SLOTS, ROWS, 256), f32),
            vmem((DEPTH, 256), bf16),
            vmem((DEPTH, 256), bf16),
            vmem((SLOTS, 2, 512, 128), f32),
            dma((3,)),
            dma((2, SLOTS, 2)),
            dma,
            dma((5,)),
            dma((5,)),
            dma,
            dma,
            dma,
        ],
        compiler_params=pltpu.CompilerParams(
            collective_id=0, has_side_effects=True, vmem_limit_bytes=VLIM
        ),
        name="irradiance",
    )(coefficients, sky, hours)


GROUP = 64


def thermal_kernel(flux_ref, air_ref, module_ref, out_ref, means):
    f32, bf16 = jnp.float32, jnp.bfloat16

    @pl.when(pl.program_id(0) == 0)
    def _():
        means[pl.ds(0, MODS), :] = jnp.zeros((MODS, WINDOW), f32)

    @pl.when(pl.program_id(0) > 0)
    def _():
        means[pl.ds(0, MODS), :] = means[pl.ds(GROUP * MODS, MODS), :]

    member = lax.broadcasted_iota(jnp.int32, (MODS, POINTS), 0) == module_ref[...]
    onehot = member.astype(bf16)
    both = jnp.concatenate([onehot, onehot], axis=1)
    for w in range(GROUP):
        stacked = jnp.concatenate(two_parts(flux_ref[w]), axis=0)
        mean = jnp.dot(both, stacked, preferred_element_type=f32) / (POINTS // MODS)
        means[pl.ds((w + 1) * MODS, MODS), :] = mean
    row = lax.broadcasted_iota(jnp.int32, (WINDOW, WINDOW), 0)
    col = lax.broadcasted_iota(jnp.int32, (WINDOW, WINDOW), 1)
    upper, lower = (row <= col).astype(bf16), (row > col).astype(bf16)
    heat = jnp.zeros((GROUP * MODS, WINDOW), f32)
    for first, weights in ((MODS, upper), (0, lower)):
        for part in two_parts(means[pl.ds(first, GROUP * MODS), :]):
            heat = heat + jnp.dot(part, weights, preferred_element_type=f32)
    heat = heat / WINDOW
    name = lax.broadcasted_iota(jnp.int32, (MODS, WINDOW), 0).astype(bf16)
    index = lax.dot_general(onehot, name, (((0,), (0,)), ((), ())), preferred_element_type=f32)
    index = index.astype(jnp.int32)
    for w in range(GROUP):
        warmth = air_ref[pl.ds(w, 1), :] + WARMUP * heat[w * MODS : (w + 1) * MODS, :]
        scale = 1.0 - LOSS * (warmth - NOMINAL)
        for r in range(POINTS // 8):
            spread = jnp.take_along_axis(scale, index[r * 8 : (r + 1) * 8, :], axis=0)
            rows = pl.ds(r * 8, 8)
            out_ref[rows, pl.ds(w * WINDOW, WINDOW)] = flux_ref[w, rows, :] * spread


def thermal_power(flux, air, modules):
    return pl.pallas_call(
        thermal_kernel,
        grid=(WINDOWS // GROUP,),
        out_shape=jax.ShapeDtypeStruct((POINTS, STEPS), jnp.float32),
        in_specs=[
            pl.BlockSpec((GROUP, POINTS, WINDOW), lambda g: (g, 0, 0)),
            pl.BlockSpec((GROUP, WINDOW), lambda g: (g, 0)),
            pl.BlockSpec((1, POINTS), lambda g: (0, 0)),
        ],
        out_specs=pl.BlockSpec((POINTS, GROUP * WINDOW), lambda g: (0, g)),
        scratch_shapes=[
            pltpu.VMEM(((GROUP + 1) * MODS, WINDOW), jnp.float32),
        ],
        compiler_params=pltpu.CompilerParams(vmem_limit_bytes=16 << 20),
        name="thermal",
    )(flux, air, modules)


def shards(coefficients, sky, outdoor_air_warmth, hour_column, module_of):
    flux = irradiance(coefficients, sky, hour_column.reshape(WINDOWS, WINDOW))
    power = thermal_power(flux, outdoor_air_warmth.reshape(WINDOWS, WINDOW), module_of.reshape(1, POINTS))
    return power.reshape(1, 1, POINTS, STEPS)


def solution(mesh):
    return jax.shard_map(
        shards,
        mesh=mesh,
        in_specs=(
            P(None, "sensor", None),
            P(None, ("hours", "sensor")),
            P(),
            P(),
            P("sensor", "hours", None),
        ),
        out_specs=P("sensor", "hours", None, None),
        check_vma=False,
    )
```

```python
import functools

import jax
import jax.numpy as jnp
from jax import lax
from jax.experimental import pallas as pl
from jax.experimental.pallas import tpu as pltpu
from jax.sharding import PartitionSpec as P

MESH = pl.DeviceIdType.MESH
PATCHES = 577
ROWS = 584
DEPTH = 640
POINTS = 64
MODS = 8
WINDOW = 128
STEPS = 32768
WINDOWS = STEPS // WINDOW
SLOTS = 16

CUTS = (424, 352)

LOSS = 0.0045
WARMUP = 50.0
NOMINAL = 25.0


def coordinates():
    h, s = lax.axis_index("hours"), lax.axis_index("sensor")
    return (h // 4) * 2 + s // 8, (s // 2) % 4, h % 4, s % 2


def along_first(place, by):
    x, y, z, c = place
    return (x + by * (1 - c)) % 4, y, (z + by * c) % 4, c


def along_second(place, by):
    x, y, z, c = place
    return x, (y + by) % 4, z, c


def along_third(place, by):
    x, y, z, c = place
    return (x + by * c) % 4, y, (z + by * (1 - c)) % 4, c


def along_x(place, by):
    x, y, z, c = place
    return (x + by) % 4, y, z, c


def sibling(place):
    x, y, z, c = place
    return x, y, z, 1 - c


def device(place):
    x, y, z, c = place
    return (x // 2) * 4 + z, ((x % 2) * 4 + y) * 2 + c


def slot_of(i, j):
    return i * 4 + j


def middle(start, stop):
    return start + (stop - start) // 16 * 8


def two_parts(value):
    high = value.astype(jnp.bfloat16)
    return high, (value - high.astype(jnp.float32)).astype(jnp.bfloat16)


def exchange(
    place, load_sem, out_ref, coef_raw, coef_own, coef_sib, coef_x, coef_high, coef_low, sky_buf, sky_high, sky_low, prod,
    sky_sems, sky_send, coef_sems, coef_send, prod_send, prod_recv, prod_own, coef_hbm,
):
    core = place[3]
    cut = CUTS[core]
    rows_of = ((0, cut), (cut, ROWS))

    def send_sky(part, i, j, second, by, which=None):
        start, stop = rows_of[part]
        if which == 0:
            stop = middle(start, stop)
        elif which == 1:
            start = middle(start, stop)
        to = slot_of(i, (j - by) % 4) if second else slot_of((i - by) % 4, j)
        rows = pl.ds(start, stop - start)
        pltpu.make_async_remote_copy(
            src_ref=sky_buf.at[slot_of(i, j), rows],
            dst_ref=sky_buf.at[to, rows],
            send_sem=sky_send,
            recv_sem=sky_sems.at[part, to, which or 0],
            device_id=device((along_second if second else along_first)(place, by % 4)),
            device_id_type=MESH,
        ).start()

    def await_sky(part, i, j):
        along, across = (i, j) if part == 0 else (j, i)
        start, stop = rows_of[part]
        slot = slot_of(i, j)

        def wait(which, start, stop):
            rows = sky_buf.at[slot, pl.ds(start, stop - start)]
            pltpu.make_async_copy(rows, rows, sky_sems.at[part, slot, which]).wait()

        if across == 2 or (across == 0 and along == 2) or (part, i) == (0, 0):
            wait(0, start, middle(start, stop))
            wait(1, middle(start, stop), stop)
        else:
            wait(0, start, stop)

    def forward_sky(part, i, j):
        along, across = (i, j) if part == 0 else (j, i)
        inner, outer = part == 1, part == 0
        if across == 0:
            if along == 3:
                send_sky(part, i, j, inner, 1, 0)
            if along == 1:
                send_sky(part, i, j, inner, -1, 1)
            send_sky(part, i, j, outer, 1)
            send_sky(part, i, j, outer, -1)
        if across == 3:
            send_sky(part, i, j, outer, 1, 0)
        if across == 1:
            send_sky(part, i, j, outer, -1, 1)

    for part, second, which in ((0, False, None), (1, True, None), (0, True, 0), (1, False, None)):
        send_sky(part, 0, 0, second, 1, which)
        send_sky(part, 0, 0, second, -1, which)

    pltpu.make_async_copy(coef_hbm, coef_raw, load_sem).wait()
    coef_own[:, pl.ds(512, 128)] = jnp.zeros((512, 128), jnp.float32)
    for tile in range(4):
        lanes = pl.ds(tile * 128, 128)
        whole = coef_raw[:, 0, lanes]
        coef_own[lanes, pl.ds(0, PATCHES)] = whole.T

    def coef_copy(src, dst, sem, to):
        return pltpu.make_async_remote_copy(
            src_ref=src, dst_ref=dst, send_sem=coef_send.at[sem], recv_sem=coef_sems.at[sem],
            device_id=device(to), device_id_type=MESH,
        )

    def row_of(place):
        return pl.ds(pl.multiple_of(device(place)[0] * 64, 64), 64)

    def put_coef(k, other, value):
        high, low = two_parts(value)
        rows = pl.ds((k * 2 + other) * 64, 64)
        coef_high[rows, :] = high
        coef_low[rows, :] = low

    def x_copies(other):
        source = (coef_own, coef_sib)[other]
        return [
            coef_copy(source.at[row_of(place)], coef_x.at[n, other], 1 + n * 2 + other, along_x(place, by))
            for n, by in ((0, 3), (1, 1))
        ]

    to_sibling = coef_copy(coef_own, coef_sib, 0, sibling(place))
    to_sibling.start()
    if core == 1:
        for copy in x_copies(0):
            copy.start()
    here = (0, 1, 2, 3) if core == 0 else (0, 2)
    for k in here:
        put_coef(k, 0, coef_own[row_of(along_third(place, k)), :])
    to_sibling.wait()
    if core == 1:
        for copy in x_copies(1):
            copy.start()
    for k in here:
        put_coef(k, 1, coef_sib[row_of(along_third(place, k)), :])

    def multiply(i, j):
        slot = slot_of(i, j)
        high, low = two_parts(sky_buf[slot, pl.ds(0, 576), :])
        sky_high[pl.ds(0, 576), :] = high
        sky_low[pl.ds(0, 576), :] = low
        high, low = two_parts(sky_buf[slot, pl.ds(576, 8), :])
        pad = jnp.zeros((8, 256), jnp.bfloat16)
        sky_high[pl.ds(576, 16), :] = jnp.concatenate([high, pad], axis=0)
        sky_low[pl.ds(576, 16), :] = jnp.concatenate([low, pad], axis=0)

        @pl.loop(0, 2)
        def _(tile):
            rows = pl.ds(pl.multiple_of(tile * 256, 256), 256)
            both = (
                jnp.dot(coef_high[rows, :], sky_low[...], preferred_element_type=jnp.float32)
                + jnp.dot(coef_low[rows, :], sky_high[...], preferred_element_type=jnp.float32)
            ) + jnp.dot(coef_high[rows, :], sky_high[...], preferred_element_type=jnp.float32)
            for half in range(2):
                prod[slot, half, rows, :] = both[:, half * 128 : (half + 1) * 128]

        owner_h, owner_s = device(along_second(along_first(place, i), j))
        windows = pl.ds((owner_h * 16 + owner_s) * 2, 2)
        for k in (2, 1, 3, 0):
            for other in range(2):
                source = prod.at[slot, :, pl.ds((k * 2 + other) * 64, 64)]
                if (k, other) == (0, 0):
                    pltpu.make_async_copy(source, out_ref.at[windows], prod_own).start()
                    continue
                to = along_third(place, k)
                pltpu.make_async_remote_copy(
                    src_ref=source,
                    dst_ref=out_ref.at[windows],
                    send_sem=prod_send,
                    recv_sem=prod_recv,
                    device_id=device(sibling(to) if other else to),
                    device_id_type=MESH,
                ).start()

    def run(*steps):
        for step in steps:
            do, *at = step
            if do == "coef":
                for other in range(2):
                    for n, copy in enumerate(x_copies(other)):
                        copy.wait()
                        put_coef(2 * n + 1, other, coef_x[n, other])
            elif do == "own":
                send_sky(0, 0, 0, True, 1, 1)
                send_sky(0, 0, 0, True, -1, 1)
            elif do == "mul":
                for i, j in at:
                    multiply(i, j)
            else:
                part = int(do[0])
                for i, j in at:
                    if "f" not in do:
                        await_sky(part, i, j)
                    if "w" not in do:
                        forward_sky(part, i, j)

    near = (
        ("1", (0, 3), (0, 1)),
        ("own",),
        ("0", (3, 0), (1, 0)),
        ("1", (3, 0), (1, 0)),
    )
    sides = ("1", (3, 3), (3, 1), (1, 3), (1, 1))
    far = (
        ("0", (1, 3), (1, 1)),
        ("mul", (1, 3), (1, 1)),
        ("1", (2, 3), (2, 1), (2, 2)),
        ("0", (2, 3), (2, 1)),
        ("mul", (2, 3), (2, 1)),
        ("0", (0, 2)),
        ("mul", (0, 2)),
        ("0", (3, 2)),
        ("mul", (3, 2)),
        ("0", (1, 2)),
        ("mul", (1, 2)),
        ("0", (2, 2)),
        ("mul", (2, 2)),
    )
    if core == 0:
        run(
            ("mul", (0, 0)),
            *near,
            ("mul", (3, 0), (1, 0)),
            ("1", (0, 2)),
            ("0w", (0, 3), (0, 1)),
            ("mul", (0, 3), (0, 1)),
            sides,
            ("0w", (3, 3), (3, 1)),
            ("mul", (3, 3), (3, 1)),
            ("0", (2, 0)),
            ("0f", (0, 3), (0, 1), (3, 3), (3, 1)),
            ("1", (2, 0)),
            ("mul", (2, 0)),
            ("1", (3, 2), (1, 2)),
            *far,
        )
    else:
        run(
            *near,
            ("coef",),
            ("mul", (0, 0), (3, 0), (1, 0)),
            ("1", (0, 2)),
            sides,
            ("0w", (0, 3), (0, 1)),
            ("mul", (0, 3), (0, 1)),
            ("0", (2, 0)),
            ("0f", (0, 3), (0, 1)),
            ("1", (2, 0)),
            ("mul", (2, 0)),
            ("0", (3, 3), (3, 1)),
            ("mul", (3, 3), (3, 1)),
            ("1", (3, 2), (1, 2)),
            *far,
        )

    def finish(ref, sem):
        pltpu.make_async_copy(ref, ref, sem).wait()

    finish(sky_buf.at[pl.ds(0, 15)], sky_send)
    finish(prod.at[pl.ds(0, 14)], prod_send)
    finish(prod.at[pl.ds(0, 2)], prod_own)
    finish(out_ref.at[pl.ds(0, WINDOWS // 8 * 7)], prod_recv)

def gather_kernel(
    coef_hbm, sky_hbm, hour_hbm, out_ref,
    coef_raw, sky_raw, hour_raw, coef_own, coef_sib, coef_x, coef_high, coef_low, sky_buf, sky_high, sky_low, prod,
    load_sem, sky_sems, sky_send, coef_sems, coef_send, prod_send, prod_recv, prod_own,
):
    place = coordinates()
    h, s = device(place)
    me = h * 16 + s
    loads = [
        pltpu.make_async_copy(sky_hbm, sky_raw, load_sem.at[0]),
        pltpu.make_async_copy(hour_hbm.at[pl.ds(pl.multiple_of((me // 4) * 8, 8), 8)], hour_raw, load_sem.at[1]),
        pltpu.make_async_copy(coef_hbm, coef_raw, load_sem.at[2]),
    ]
    for load in loads:
        load.start()

    partners = [along_second(place, 1), along_second(place, 3), sibling(place)]
    for k in (1, 2, 3):
        for partner in (along_third(place, k), along_first(place, k)):
            partners += [partner, sibling(partner)]
    barrier = pltpu.get_barrier_semaphore()
    for partner in partners:
        pl.semaphore_signal(barrier, inc=1, device_id=device(partner), device_id_type=MESH)

    loads[0].wait()
    loads[1].wait()
    sky_parts = two_parts(sky_raw[...])
    sky_buf[0, pl.ds(PATCHES - 1, 8), :] = jnp.zeros((8, 256), jnp.float32)
    for half in range(2):
        column = hour_raw[pl.ds((me % 4) * 2 + half, 1), :] - me * 256
        chosen = (lax.broadcasted_iota(jnp.int32, (256, 128), 0) == column).astype(jnp.bfloat16)
        ordered = sum(jnp.dot(part, chosen, preferred_element_type=jnp.float32) for part in sky_parts)
        sky_buf[0, pl.ds(0, PATCHES), pl.ds(half * 128, 128)] = ordered
    sky_high[pl.ds(576, 64), :] = jnp.zeros((64, 256), jnp.bfloat16)
    sky_low[pl.ds(576, 64), :] = jnp.zeros((64, 256), jnp.bfloat16)
    pl.semaphore_wait(barrier, len(partners))


    for core in range(2):
        @pl.when(place[3] == core)
        def _(core=core):
            exchange(
                (*place[:3], core), load_sem.at[2], out_ref, coef_raw, coef_own, coef_sib, coef_x, coef_high, coef_low,
                sky_buf, sky_high, sky_low, prod, sky_sems, sky_send, coef_sems, coef_send, prod_send, prod_recv, prod_own, coef_hbm,
            )


def irradiance(coefficients, sky, hours):
    coefficients, sky, hours = [pltpu.with_memory_space_constraint(a, pltpu.HBM) for a in (coefficients, sky, hours)]
    f32, bf16 = jnp.float32, jnp.bfloat16
    vmem, dma = pltpu.VMEM, pltpu.SemaphoreType.DMA
    return pl.pallas_call(
        gather_kernel,
        out_shape=jax.ShapeDtypeStruct((WINDOWS, POINTS, WINDOW), f32),
        in_specs=[pl.BlockSpec(memory_space=pltpu.HBM)] * 3,
        out_specs=pl.BlockSpec(memory_space=pl.ANY),
        scratch_shapes=[
            vmem((PATCHES, 1, 512), f32),
            vmem((PATCHES, 256), f32),
            vmem((8, 128), jnp.int32),
            vmem((512, DEPTH), f32),
            vmem((512, DEPTH), f32),
            vmem((2, 2, 64, DEPTH), f32),
            vmem((512, DEPTH), bf16),
            vmem((512, DEPTH), bf16),
            vmem((SLOTS, ROWS, 256), f32),
            vmem((DEPTH, 256), bf16),
            vmem((DEPTH, 256), bf16),
            vmem((SLOTS, 2, 512, 128), f32),
            dma((3,)),
            dma((2, SLOTS, 2)),
            dma,
            dma((5,)),
            dma((5,)),
            dma,
            dma,
            dma,
        ],
        compiler_params=pltpu.CompilerParams(
            collective_id=0, has_side_effects=True, vmem_limit_bytes=32 << 20
        ),
        name="irradiance",
    )(coefficients, sky, hours)


GROUP = 32
BUFFERS = 4


def thermal_kernel(flux_ref, air_ref, module_ref, out_hbm, means, buffers, sems):
    f32, bf16 = jnp.float32, jnp.bfloat16
    onehot = (lax.broadcasted_iota(jnp.int32, (MODS, POINTS), 0) == module_ref[...]).astype(bf16)
    both = jnp.concatenate([onehot, onehot], axis=1)
    none = jnp.zeros_like(both)
    pair = jnp.concatenate([jnp.concatenate([both, none], axis=1), jnp.concatenate([none, both], axis=1)], axis=0)
    row = lax.broadcasted_iota(jnp.int32, (WINDOW, WINDOW), 0)
    col = lax.broadcasted_iota(jnp.int32, (WINDOW, WINDOW), 1)
    summing = jnp.concatenate([(row <= col).astype(bf16), (row > col).astype(bf16)], axis=0)
    name = lax.broadcasted_iota(jnp.int32, (MODS, WINDOW), 0).astype(bf16)
    index = lax.dot_general(onehot, name, (((0,), (0,)), ((), ())), preferred_element_type=f32)
    index = index.astype(jnp.int32)
    means[pl.ds(0, MODS), :] = jnp.zeros((MODS, WINDOW), f32)

    def copy(group):
        slot = group % BUFFERS
        columns = pl.ds(group * GROUP * WINDOW, GROUP * WINDOW)
        return pltpu.make_async_copy(buffers.at[slot], out_hbm.at[:, columns], sems.at[slot])

    groups = WINDOWS // GROUP
    for group in range(groups):
        if group >= BUFFERS:
            copy(group - BUFFERS).wait()
        start = group * GROUP
        for w in range(start, start + GROUP, 2):
            parts = jnp.concatenate([*two_parts(flux_ref[w]), *two_parts(flux_ref[w + 1])], axis=0)
            mean = jnp.dot(pair, parts, preferred_element_type=f32) / (POINTS // MODS)
            means[pl.ds((w + 1) * MODS, 2 * MODS), :] = mean
        now = two_parts(means[pl.ds((start + 1) * MODS, GROUP * MODS), :])
        before = two_parts(means[pl.ds(start * MODS, GROUP * MODS), :])
        heat = jnp.zeros((GROUP * MODS, WINDOW), f32)
        for part in range(2):
            windows = jnp.concatenate([now[part], before[part]], axis=1)
            heat = heat + jnp.dot(windows, summing, preferred_element_type=f32)
        heat = heat / WINDOW
        for w in range(GROUP):
            warmth = air_ref[pl.ds(start + w, 1), :] + WARMUP * heat[w * MODS : (w + 1) * MODS, :]
            scale = 1.0 - LOSS * (warmth - NOMINAL)
            for r in range(POINTS // 8):
                rows = pl.ds(r * 8, 8)
                spread = jnp.take_along_axis(scale, index[r * 8 : (r + 1) * 8, :], axis=0)
                buffers[group % BUFFERS, rows, pl.ds(w * WINDOW, WINDOW)] = flux_ref[start + w, rows, :] * spread
        copy(group).start()
    for group in range(groups - BUFFERS, groups):
        copy(group).wait()


def thermal_power(flux, air, modules):
    return pl.pallas_call(
        thermal_kernel,
        out_shape=jax.ShapeDtypeStruct((POINTS, STEPS), jnp.float32),
        in_specs=[pl.BlockSpec(memory_space=pltpu.VMEM)] * 3,
        out_specs=pl.BlockSpec(memory_space=pl.ANY),
        scratch_shapes=[
            pltpu.VMEM(((WINDOWS + 1) * MODS, WINDOW), jnp.float32),
            pltpu.VMEM((BUFFERS, POINTS, GROUP * WINDOW), jnp.float32),
            pltpu.SemaphoreType.DMA((BUFFERS,)),
        ],
        compiler_params=pltpu.CompilerParams(vmem_limit_bytes=24 << 20),
        name="thermal",
    )(flux, air, modules)


def shards(coefficients, sky, outdoor_air_warmth, hour_column, module_of):
    flux = irradiance(coefficients, sky, hour_column.reshape(WINDOWS, WINDOW))
    power = thermal_power(flux, outdoor_air_warmth.reshape(WINDOWS, WINDOW), module_of.reshape(1, POINTS))
    return power.reshape(1, 1, POINTS, STEPS)


def solution(mesh):
    return jax.shard_map(
        shards,
        mesh=mesh,
        in_specs=(
            P(None, "sensor", None),
            P(None, ("hours", "sensor")),
            P(),
            P(),
            P("sensor", "hours", None),
        ),
        out_specs=P("sensor", "hours", None, None),
        check_vma=False,
    )
```

```python
import functools

import jax
import jax.numpy as jnp
from jax import lax
from jax.experimental import pallas as pl
from jax.experimental.pallas import tpu as pltpu
from jax.sharding import PartitionSpec as P

MESH = pl.DeviceIdType.MESH
PATCHES = 577
ROWS = 584
DEPTH = 640
POINTS = 64
MODS = 8
WINDOW = 128
STEPS = 32768
WINDOWS = STEPS // WINDOW
SLOTS = 16

X0, X1, Y0, Y1, Z0, Z1 = range(6)
SIDES = ((Z0, Z1, X0), (X1, Y0, Y1))
PIECES = ((0, 200), (200, 392), (392, 584))


def bits(*dimensions):
    return sum(1 << d for d in dimensions)


class Plan:
    def __init__(self, core):
        self.bridge, self.cube = SIDES[core], SIDES[1 - core]
        self.far = bits(*self.bridge)
        near = [bits(*(d for n, d in enumerate(self.cube) if at >> n & 1)) for at in range(8)]
        self.nodes = near + [self.far | node for node in near]
        self.trees = [self.tree_of(piece) for piece in range(3)]
        self.relays = [node for tree in self.trees for node, _, _ in tree[:2]]

    def orders(self, piece):
        return self.cube[piece:] + self.cube[:piece], self.bridge[piece:] + self.bridge[:piece]

    def tree_of(self, piece):
        (a, b, c), (p, q, r) = self.orders(piece)
        tree = [(bits(p), 0, p), (bits(p, q), bits(p), q), (self.far, bits(p, q), r)]
        for far in (0, self.far):
            for node, parent, d in (
                (bits(a), 0, a), (bits(b), 0, b), (bits(c), 0, c), (bits(a, b), bits(a), b), (bits(a, c), bits(a), c),
                (bits(b, c), bits(b), c), (bits(a, b, c), bits(a, b), c),
            ):
                tree.append((far | node, far | parent, d))
        return tree


LOSS = 0.0045
WARMUP = 50.0
NOMINAL = 25.0


def coordinates():
    h, s = lax.axis_index("hours"), lax.axis_index("sensor")
    return (h // 4) * 2 + s // 8, (s // 2) % 4, h % 4, s % 2


def flipped(place, dimension):
    moved = list(place)
    at = moved[dimension // 2]
    moved[dimension // 2] = 3 - at if dimension % 2 else at + 1 - 2 * (at % 2)
    return tuple(moved)


def node_of(place, node):
    for dimension in range(6):
        if node >> dimension & 1:
            place = flipped(place, dimension)
    return place


def sibling(place):
    x, y, z, c = place
    return x, y, z, 1 - c


def device(place):
    x, y, z, c = place
    return (x // 2) * 4 + z, ((x % 2) * 4 + y) * 2 + c


def two_parts(value):
    high = value.astype(jnp.bfloat16)
    return high, (value - high.astype(jnp.float32)).astype(jnp.bfloat16)


def exchange(
    place, load_sem, out_ref, coef_raw, coef_own, coef_sib, coef_next, coef_high, coef_low, sky_buf, relay, sky_high, sky_low, prod,
    sky_sems, sky_send, coef_sems, coef_send, prod_send, prod_recv, prod_own, coef_hbm,
):
    core = place[3]
    plan = Plan(core)
    nodes, relays, far, orders = plan.nodes, plan.relays, plan.far, plan.orders

    def chunk(node, piece):
        start, stop = PIECES[piece]
        if node in nodes:
            return sky_buf.at[nodes.index(node), pl.ds(start, stop - start)]
        return relay.at[relays.index(node), pl.ds(0, stop - start)]

    def sem_of(node, piece):
        return sky_sems.at[(nodes + relays).index(node), piece]

    def forward_sky(node, piece, among=range(6)):
        for to, parent, dimension in plan.trees[piece]:
            if parent == node and dimension in among:
                pltpu.make_async_remote_copy(
                    src_ref=chunk(node, piece),
                    dst_ref=chunk(to, piece),
                    send_sem=sky_send.at[int(to & far == far)],
                    recv_sem=sem_of(to, piece),
                    device_id=device(flipped(place, dimension)),
                    device_id_type=MESH,
                ).start()

    def await_sky(node, piece):
        rows = chunk(node, piece)
        pltpu.make_async_copy(rows, rows, sem_of(node, piece)).wait()

    def spread_sky(node, rounds=(0, 1, 2)):
        for n in rounds:
            for piece in range(3):
                forward_sky(node, piece, orders(piece)[0][n : n + 1])

    for piece in range(3):
        forward_sky(0, piece, plan.bridge)
    spread_sky(0, (0,))

    pltpu.make_async_copy(coef_hbm, coef_raw, load_sem).wait()
    coef_own[:, pl.ds(512, 128)] = jnp.zeros((512, 128), jnp.float32)
    for tile in range(4):
        lanes = pl.ds(tile * 128, 128)
        whole = coef_raw[:, 0, lanes]
        coef_own[lanes, pl.ds(0, PATCHES)] = whole.T

    def coef_copy(src, dst, sem, to, other):
        return pltpu.make_async_remote_copy(
            src_ref=src, dst_ref=dst, send_sem=coef_send.at[sem], recv_sem=coef_sems.at[sem, other],
            device_id=device(to), device_id_type=MESH,
        )

    def row_of(place):
        return pl.ds(pl.multiple_of(device(place)[0] * 64, 64), 64)

    def put_coef(block, other, value):
        high, low = two_parts(value)
        rows = pl.ds(block * 128 + other * 64, 64)
        coef_high[rows, :] = high
        coef_low[rows, :] = low

    own = coef_own.at[row_of(place)]

    def next_copy(dimension):
        to = flipped(place, dimension)
        server = 0 if dimension in SIDES[0] else 1
        return coef_copy(own, coef_next.at[SIDES[server].index(dimension), core], dimension, (*to[:3], server), core)

    sent = [next_copy(dimension) for dimension in (X0, X1, Y0, Y1)]
    for copy in sent:
        copy.start()
    spread_sky(0, (1, 2))
    local = [place] if core == 0 else [place, flipped(place, Z0), flipped(place, Z1)]
    to_sibling = [
        coef_copy(coef_own.at[row_of(at)], coef_sib.at[block], 4 + block, sibling(place), 0) for block, at in enumerate(local)
    ]
    for copy in to_sibling:
        copy.start()
    here = (place, flipped(place, Z0), flipped(place, Z1)) if core == 0 else (place,)
    for block, at in enumerate(here):
        put_coef(block, 0, coef_own[row_of(at), :])
    for copy in to_sibling:
        copy.wait_send()
    for block in range(len(here)):
        pltpu.make_async_copy(coef_sib.at[block], coef_sib.at[block], coef_sems.at[4 + block, 0]).wait()
        put_coef(block, 1, coef_sib[block])

    def multiply(node):
        slot = nodes.index(node)
        high, low = two_parts(sky_buf[slot, pl.ds(0, 576), :])
        sky_high[pl.ds(0, 576), :] = high
        sky_low[pl.ds(0, 576), :] = low
        high, low = two_parts(sky_buf[slot, pl.ds(576, 8), :])
        pad = jnp.zeros((8, 256), jnp.bfloat16)
        sky_high[pl.ds(576, 16), :] = jnp.concatenate([high, pad], axis=0)
        sky_low[pl.ds(576, 16), :] = jnp.concatenate([low, pad], axis=0)

        @pl.loop(0, 2)
        def _(tile):
            rows = pl.ds(pl.multiple_of(tile * 256, 256), 256)
            both = (
                jnp.dot(coef_high[rows, :], sky_low[...], preferred_element_type=jnp.float32)
                + jnp.dot(coef_low[rows, :], sky_high[...], preferred_element_type=jnp.float32)
            ) + jnp.dot(coef_high[rows, :], sky_high[...], preferred_element_type=jnp.float32)
            for half in range(2):
                prod[slot, half, rows, :] = both[:, half * 128 : (half + 1) * 128]

        owner_h, owner_s = device(node_of(place, node))
        windows = pl.ds((owner_h * 16 + owner_s) * 2, 2)
        for block in (3, 1, 2, 0):
            to = flipped(place, plan.bridge[block - 1]) if block else place
            for other in range(2):
                source = prod.at[slot, :, pl.ds(block * 128 + other * 64, 64)]
                if (block, other) == (0, 0):
                    pltpu.make_async_copy(source, out_ref.at[windows], prod_own).start()
                    continue
                pltpu.make_async_remote_copy(
                    src_ref=source,
                    dst_ref=out_ref.at[windows],
                    send_sem=prod_send,
                    recv_sem=prod_recv,
                    device_id=device(sibling(to) if other else to),
                    device_id_type=MESH,
                ).start()

    def take(pick):
        for piece in range(3):
            node = pick(*orders(piece))
            await_sky(node, piece)
            if node != far:
                forward_sky(node, piece)

    def multiply_all(*nodes):
        for node in nodes:
            multiply(node)

    a, b, c = plan.cube
    singles = (bits(a), bits(b), bits(c))
    doubles = (bits(a, b), bits(b, c), bits(a, c))
    take(lambda cube, bridge: bits(bridge[0]))
    take(lambda cube, bridge: bits(cube[0]))
    for copy in sent:
        copy.wait_send()
    for n, dimension in enumerate(plan.bridge):
        if dimension in (Z0, Z1):
            continue
        for other in range(2):
            came = coef_next.at[n, core if other == 0 else 1 - core]
            sem = core if other == 0 else 1 - core
            pltpu.make_async_copy(came, came, coef_sems.at[dimension, sem]).wait()
            put_coef(1 + n, other, came[...])
    take(lambda cube, bridge: bits(bridge[0], bridge[1]))
    multiply_all(0)
    take(lambda cube, bridge: bits(cube[1]))
    take(lambda cube, bridge: bits(cube[2]))
    take(lambda cube, bridge: far)
    spread_sky(far)
    multiply_all(*singles)
    take(lambda cube, bridge: bits(cube[0], cube[1]))
    multiply_all(far)
    take(lambda cube, bridge: bits(cube[0], cube[2]))
    take(lambda cube, bridge: bits(cube[1], cube[2]))
    take(lambda cube, bridge: far | bits(cube[0]))
    multiply_all(*doubles)
    take(lambda cube, bridge: bits(*cube))
    take(lambda cube, bridge: far | bits(cube[1]))
    multiply_all(bits(*plan.cube))
    take(lambda cube, bridge: far | bits(cube[2]))
    multiply_all(*(far | node for node in singles))
    take(lambda cube, bridge: far | bits(cube[0], cube[1]))
    take(lambda cube, bridge: far | bits(cube[0], cube[2]))
    take(lambda cube, bridge: far | bits(cube[1], cube[2]))
    multiply_all(*(far | node for node in doubles))
    take(lambda cube, bridge: far | bits(*cube))
    multiply_all(far | bits(*plan.cube))

    def finish(ref, sem):
        pltpu.make_async_copy(ref, ref, sem).wait()

    finish(sky_buf.at[pl.ds(0, 9)], sky_send.at[0])
    finish(sky_buf.at[pl.ds(0, 8)], sky_send.at[1])
    finish(prod.at[pl.ds(0, 14)], prod_send)
    finish(prod.at[pl.ds(0, 2)], prod_own)
    finish(out_ref.at[pl.ds(0, WINDOWS // 8 * 7)], prod_recv)


def gather_kernel(
    coef_hbm, sky_hbm, hour_hbm, out_ref,
    coef_raw, sky_raw, hour_raw, coef_own, coef_sib, coef_next, coef_high, coef_low, sky_buf, relay, sky_high, sky_low, prod,
    load_sem, sky_sems, sky_send, coef_sems, coef_send, prod_send, prod_recv, prod_own,
):
    place = coordinates()
    h, s = device(place)
    me = h * 16 + s
    loads = [
        pltpu.make_async_copy(sky_hbm, sky_raw, load_sem.at[0]),
        pltpu.make_async_copy(hour_hbm.at[pl.ds(pl.multiple_of((me // 4) * 8, 8), 8)], hour_raw, load_sem.at[1]),
        pltpu.make_async_copy(coef_hbm, coef_raw, load_sem.at[2]),
    ]
    for load in loads:
        load.start()

    partners = [sibling(place)]
    for dimension in range(6):
        partners += [flipped(place, dimension), sibling(flipped(place, dimension))]
    barrier = pltpu.get_barrier_semaphore()
    for partner in partners:
        pl.semaphore_signal(barrier, inc=1, device_id=device(partner), device_id_type=MESH)

    loads[0].wait()
    loads[1].wait()
    sky_parts = two_parts(sky_raw[...])
    sky_buf[0, pl.ds(PATCHES - 1, 8), :] = jnp.zeros((8, 256), jnp.float32)
    for half in range(2):
        column = hour_raw[pl.ds((me % 4) * 2 + half, 1), :] - me * 256
        chosen = (lax.broadcasted_iota(jnp.int32, (256, 128), 0) == column).astype(jnp.bfloat16)
        ordered = sum(jnp.dot(part, chosen, preferred_element_type=jnp.float32) for part in sky_parts)
        sky_buf[0, pl.ds(0, PATCHES), pl.ds(half * 128, 128)] = ordered
    sky_high[pl.ds(576, 64), :] = jnp.zeros((64, 256), jnp.bfloat16)
    sky_low[pl.ds(576, 64), :] = jnp.zeros((64, 256), jnp.bfloat16)
    pl.semaphore_wait(barrier, len(partners))


    for core in range(2):
        @pl.when(place[3] == core)
        def _(core=core):
            exchange(
                (*place[:3], core), load_sem.at[2], out_ref, coef_raw, coef_own, coef_sib, coef_next, coef_high, coef_low,
                sky_buf, relay, sky_high, sky_low, prod, sky_sems, sky_send, coef_sems, coef_send, prod_send, prod_recv,
                prod_own, coef_hbm,
            )


def irradiance(coefficients, sky, hours):
    coefficients, sky, hours = [pltpu.with_memory_space_constraint(a, pltpu.HBM) for a in (coefficients, sky, hours)]
    f32, bf16 = jnp.float32, jnp.bfloat16
    vmem, dma = pltpu.VMEM, pltpu.SemaphoreType.DMA
    return pl.pallas_call(
        gather_kernel,
        out_shape=jax.ShapeDtypeStruct((WINDOWS, POINTS, WINDOW), f32),
        in_specs=[pl.BlockSpec(memory_space=pltpu.HBM)] * 3,
        out_specs=pl.BlockSpec(memory_space=pl.ANY),
        scratch_shapes=[
            vmem((PATCHES, 1, 512), f32),
            vmem((PATCHES, 256), f32),
            vmem((8, 128), jnp.int32),
            vmem((512, DEPTH), f32),
            vmem((3, 64, DEPTH), f32),
            vmem((3, 2, 64, DEPTH), f32),
            vmem((512, DEPTH), bf16),
            vmem((512, DEPTH), bf16),
            vmem((SLOTS, ROWS, 256), f32),
            vmem((6, 200, 256), f32),
            vmem((DEPTH, 256), bf16),
            vmem((DEPTH, 256), bf16),
            vmem((SLOTS, 2, 512, 128), f32),
            dma((3,)),
            dma((SLOTS + 6, 3)),
            dma((2,)),
            dma((7, 2)),
            dma((7,)),
            dma,
            dma,
            dma,
        ],
        compiler_params=pltpu.CompilerParams(
            collective_id=0, has_side_effects=True, vmem_limit_bytes=32 << 20
        ),
        name="irradiance",
    )(coefficients, sky, hours)


GROUP = 32
BUFFERS = 4


def thermal_kernel(flux_ref, air_ref, module_ref, out_hbm, means, buffers, sems):
    f32, bf16 = jnp.float32, jnp.bfloat16
    onehot = (lax.broadcasted_iota(jnp.int32, (MODS, POINTS), 0) == module_ref[...]).astype(bf16)
    both = jnp.concatenate([onehot, onehot], axis=1)
    none = jnp.zeros_like(both)
    pair = jnp.concatenate([jnp.concatenate([both, none], axis=1), jnp.concatenate([none, both], axis=1)], axis=0)
    row = lax.broadcasted_iota(jnp.int32, (WINDOW, WINDOW), 0)
    col = lax.broadcasted_iota(jnp.int32, (WINDOW, WINDOW), 1)
    summing = jnp.concatenate([(row <= col).astype(bf16), (row > col).astype(bf16)], axis=0)
    name = lax.broadcasted_iota(jnp.int32, (MODS, WINDOW), 0).astype(bf16)
    index = lax.dot_general(onehot, name, (((0,), (0,)), ((), ())), preferred_element_type=f32)
    index = index.astype(jnp.int32)
    means[pl.ds(0, MODS), :] = jnp.zeros((MODS, WINDOW), f32)

    def copy(group):
        slot = group % BUFFERS
        columns = pl.ds(group * GROUP * WINDOW, GROUP * WINDOW)
        return pltpu.make_async_copy(buffers.at[slot], out_hbm.at[:, columns], sems.at[slot])

    groups = WINDOWS // GROUP
    for group in range(groups):
        if group >= BUFFERS:
            copy(group - BUFFERS).wait()
        start = group * GROUP
        for w in range(start, start + GROUP, 2):
            parts = jnp.concatenate([*two_parts(flux_ref[w]), *two_parts(flux_ref[w + 1])], axis=0)
            mean = jnp.dot(pair, parts, preferred_element_type=f32) / (POINTS // MODS)
            means[pl.ds((w + 1) * MODS, 2 * MODS), :] = mean
        now = two_parts(means[pl.ds((start + 1) * MODS, GROUP * MODS), :])
        before = two_parts(means[pl.ds(start * MODS, GROUP * MODS), :])
        heat = jnp.zeros((GROUP * MODS, WINDOW), f32)
        for part in range(2):
            windows = jnp.concatenate([now[part], before[part]], axis=1)
            heat = heat + jnp.dot(windows, summing, preferred_element_type=f32)
        heat = heat / WINDOW
        for w in range(GROUP):
            warmth = air_ref[pl.ds(start + w, 1), :] + WARMUP * heat[w * MODS : (w + 1) * MODS, :]
            scale = 1.0 - LOSS * (warmth - NOMINAL)
            for r in range(POINTS // 8):
                rows = pl.ds(r * 8, 8)
                spread = jnp.take_along_axis(scale, index[r * 8 : (r + 1) * 8, :], axis=0)
                buffers[group % BUFFERS, rows, pl.ds(w * WINDOW, WINDOW)] = flux_ref[start + w, rows, :] * spread
        copy(group).start()
    for group in range(groups - BUFFERS, groups):
        copy(group).wait()


def thermal_power(flux, air, modules):
    return pl.pallas_call(
        thermal_kernel,
        out_shape=jax.ShapeDtypeStruct((POINTS, STEPS), jnp.float32),
        in_specs=[pl.BlockSpec(memory_space=pltpu.VMEM)] * 3,
        out_specs=pl.BlockSpec(memory_space=pl.ANY),
        scratch_shapes=[
            pltpu.VMEM(((WINDOWS + 1) * MODS, WINDOW), jnp.float32),
            pltpu.VMEM((BUFFERS, POINTS, GROUP * WINDOW), jnp.float32),
            pltpu.SemaphoreType.DMA((BUFFERS,)),
        ],
        compiler_params=pltpu.CompilerParams(vmem_limit_bytes=24 << 20),
        name="thermal",
    )(flux, air, modules)


def shards(coefficients, sky, outdoor_air_warmth, hour_column, module_of):
    flux = irradiance(coefficients, sky, hour_column.reshape(WINDOWS, WINDOW))
    power = thermal_power(flux, outdoor_air_warmth.reshape(WINDOWS, WINDOW), module_of.reshape(1, POINTS))
    return power.reshape(1, 1, POINTS, STEPS)


def solution(mesh):
    return jax.shard_map(
        shards,
        mesh=mesh,
        in_specs=(
            P(None, "sensor", None),
            P(None, ("hours", "sensor")),
            P(),
            P(),
            P("sensor", "hours", None),
        ),
        out_specs=P("sensor", "hours", None, None),
        check_vma=False,
    )
```

```python
import functools

import jax
import jax.numpy as jnp
from jax import lax
from jax.experimental import pallas as pl
from jax.experimental.pallas import tpu as pltpu
from jax.sharding import PartitionSpec as P

MESH = pl.DeviceIdType.MESH
PATCHES = 577
ROWS = 584
DEPTH = 640
POINTS = 64
MODS = 8
WINDOW = 128
STEPS = 32768
WINDOWS = STEPS // WINDOW
SLOTS = 16

X0, X1, Y0, Y1, Z0, Z1 = range(6)
SIDES = ((Z0, Z1, X0), (X1, Y0, Y1))
PIECES = ((0, 200), (200, 392), (392, 584))


def bits(*dimensions):
    return sum(1 << d for d in dimensions)


class Plan:
    def __init__(self, core):
        self.bridge, self.cube = SIDES[core], SIDES[1 - core]
        self.far = bits(*self.bridge)
        near = [bits(*(d for n, d in enumerate(self.cube) if at >> n & 1)) for at in range(8)]
        self.nodes = near + [self.far | node for node in near]
        self.trees = [self.tree_of(piece) for piece in range(3)]
        self.relays = [node for tree in self.trees for node, _, _ in tree[:2]]

    def orders(self, piece):
        return self.cube[piece:] + self.cube[:piece], self.bridge[piece:] + self.bridge[:piece]

    def tree_of(self, piece):
        (a, b, c), (p, q, r) = self.orders(piece)
        tree = [(bits(p), 0, p), (bits(p, q), bits(p), q), (self.far, bits(p, q), r)]
        for far in (0, self.far):
            for node, parent, d in (
                (bits(a), 0, a), (bits(b), 0, b), (bits(c), 0, c), (bits(a, b), bits(a), b), (bits(a, c), bits(a), c),
                (bits(b, c), bits(b), c), (bits(a, b, c), bits(a, b), c),
            ):
                tree.append((far | node, far | parent, d))
        return tree


LOSS = 0.0045
WARMUP = 50.0
NOMINAL = 25.0


def coordinates():
    h, s = lax.axis_index("hours"), lax.axis_index("sensor")
    return (h // 4) * 2 + s // 8, (s // 2) % 4, h % 4, s % 2


def flipped(place, dimension):
    moved = list(place)
    at = moved[dimension // 2]
    moved[dimension // 2] = 3 - at if dimension % 2 else at + 1 - 2 * (at % 2)
    return tuple(moved)


def node_of(place, node):
    for dimension in range(6):
        if node >> dimension & 1:
            place = flipped(place, dimension)
    return place


def sibling(place):
    x, y, z, c = place
    return x, y, z, 1 - c


def device(place):
    x, y, z, c = place
    return (x // 2) * 4 + z, ((x % 2) * 4 + y) * 2 + c


def two_parts(value):
    high = value.astype(jnp.bfloat16)
    return high, (value - high.astype(jnp.float32)).astype(jnp.bfloat16)


def exchange(
    place, load_sem, out_ref, coef_raw, coef_own, coef_sib, coef_next, coef_high, coef_low, sky_buf, relay, sky_high, sky_low, prod,
    sky_sems, sky_send, coef_sems, coef_send, prod_send, prod_recv, prod_own, coef_hbm,
):
    core = place[3]
    plan = Plan(core)
    nodes, relays, far, orders = plan.nodes, plan.relays, plan.far, plan.orders

    def chunk(node, piece):
        start, stop = PIECES[piece]
        if node in nodes:
            return sky_buf.at[nodes.index(node), pl.ds(start, stop - start)]
        return relay.at[relays.index(node), pl.ds(0, stop - start)]

    def sem_of(node, piece):
        return sky_sems.at[(nodes + relays).index(node), piece]

    def forward_sky(node, piece, among=range(6)):
        for to, parent, dimension in plan.trees[piece]:
            if parent == node and dimension in among:
                pltpu.make_async_remote_copy(
                    src_ref=chunk(node, piece),
                    dst_ref=chunk(to, piece),
                    send_sem=sky_send.at[int(to & far == far)],
                    recv_sem=sem_of(to, piece),
                    device_id=device(flipped(place, dimension)),
                    device_id_type=MESH,
                ).start()

    def await_sky(node, piece):
        rows = chunk(node, piece)
        pltpu.make_async_copy(rows, rows, sem_of(node, piece)).wait()

    def spread_sky(node, rounds=(0, 1, 2)):
        for n in rounds:
            for piece in range(3):
                forward_sky(node, piece, orders(piece)[0][n : n + 1])

    for piece in range(3):
        forward_sky(0, piece, plan.bridge)
    spread_sky(0, (0,))

    pltpu.make_async_copy(coef_hbm, coef_raw, load_sem).wait()
    coef_own[:, pl.ds(512, 128)] = jnp.zeros((512, 128), jnp.float32)
    for tile in range(4):
        lanes = pl.ds(tile * 128, 128)
        whole = coef_raw[:, 0, lanes]
        coef_own[lanes, pl.ds(0, PATCHES)] = whole.T

    def coef_copy(src, dst, sem, to, other):
        return pltpu.make_async_remote_copy(
            src_ref=src, dst_ref=dst, send_sem=coef_send.at[sem], recv_sem=coef_sems.at[sem, other],
            device_id=device(to), device_id_type=MESH,
        )

    def row_of(place):
        return pl.ds(pl.multiple_of(device(place)[0] * 64, 64), 64)

    def put_coef(block, other, value):
        high, low = two_parts(value)
        rows = pl.ds(block * 128 + other * 64, 64)
        coef_high[rows, :] = high
        coef_low[rows, :] = low

    own = coef_own.at[row_of(place)]

    def next_copy(dimension):
        to = flipped(place, dimension)
        server = 0 if dimension in SIDES[0] else 1
        return coef_copy(own, coef_next.at[SIDES[server].index(dimension), core], dimension, (*to[:3], server), core)

    sent = [next_copy(dimension) for dimension in (X0, X1, Y0, Y1)]
    for copy in sent:
        copy.start()
    spread_sky(0, (1, 2))
    local = [place] if core == 0 else [place, flipped(place, Z0), flipped(place, Z1)]
    to_sibling = [
        coef_copy(coef_own.at[row_of(at)], coef_sib.at[block], 4 + block, sibling(place), 0) for block, at in enumerate(local)
    ]
    for copy in to_sibling:
        copy.start()
    here = (place, flipped(place, Z0), flipped(place, Z1)) if core == 0 else (place,)
    for block, at in enumerate(here):
        put_coef(block, 0, coef_own[row_of(at), :])
    for copy in to_sibling:
        copy.wait_send()
    for block in range(len(here)):
        pltpu.make_async_copy(coef_sib.at[block], coef_sib.at[block], coef_sems.at[4 + block, 0]).wait()
        put_coef(block, 1, coef_sib[block])

    def multiply(node):
        slot = nodes.index(node)
        high, low = two_parts(sky_buf[slot, pl.ds(0, 576), :])
        sky_high[pl.ds(0, 576), :] = high
        sky_low[pl.ds(0, 576), :] = low
        high, low = two_parts(sky_buf[slot, pl.ds(576, 8), :])
        pad = jnp.zeros((8, 256), jnp.bfloat16)
        sky_high[pl.ds(576, 16), :] = jnp.concatenate([high, pad], axis=0)
        sky_low[pl.ds(576, 16), :] = jnp.concatenate([low, pad], axis=0)

        @pl.loop(0, 2)
        def _(tile):
            rows = pl.ds(pl.multiple_of(tile * 256, 256), 256)
            both = (
                jnp.dot(coef_high[rows, :], sky_low[...], preferred_element_type=jnp.float32)
                + jnp.dot(coef_low[rows, :], sky_high[...], preferred_element_type=jnp.float32)
            ) + jnp.dot(coef_high[rows, :], sky_high[...], preferred_element_type=jnp.float32)
            for half in range(2):
                prod[slot, half, rows, :] = both[:, half * 128 : (half + 1) * 128]

        owner_h, owner_s = device(node_of(place, node))
        windows = pl.ds((owner_h * 16 + owner_s) * 2, 2)
        for block in (3, 1, 2, 0):
            to = flipped(place, plan.bridge[block - 1]) if block else place
            for other in range(2):
                source = prod.at[slot, :, pl.ds(block * 128 + other * 64, 64)]
                if (block, other) == (0, 0):
                    pltpu.make_async_copy(source, out_ref.at[windows], prod_own).start()
                    continue
                pltpu.make_async_remote_copy(
                    src_ref=source,
                    dst_ref=out_ref.at[windows],
                    send_sem=prod_send,
                    recv_sem=prod_recv,
                    device_id=device(sibling(to) if other else to),
                    device_id_type=MESH,
                ).start()

    def take(pick):
        for piece in range(3):
            node = pick(*orders(piece))
            await_sky(node, piece)
            if node != far:
                forward_sky(node, piece)

    def multiply_all(*nodes):
        for node in nodes:
            multiply(node)

    a, b, c = plan.cube
    singles = (bits(a), bits(b), bits(c))
    doubles = (bits(a, b), bits(b, c), bits(a, c))
    take(lambda cube, bridge: bits(bridge[0]))
    take(lambda cube, bridge: bits(cube[0]))
    for copy in sent:
        copy.wait_send()
    for n, dimension in enumerate(plan.bridge):
        if dimension in (Z0, Z1):
            continue
        for other in range(2):
            came = coef_next.at[n, core if other == 0 else 1 - core]
            sem = core if other == 0 else 1 - core
            pltpu.make_async_copy(came, came, coef_sems.at[dimension, sem]).wait()
            put_coef(1 + n, other, came[...])
    take(lambda cube, bridge: bits(bridge[0], bridge[1]))
    multiply_all(0)
    take(lambda cube, bridge: bits(cube[1]))
    take(lambda cube, bridge: bits(cube[2]))
    take(lambda cube, bridge: far)
    spread_sky(far)
    multiply_all(*singles)
    take(lambda cube, bridge: bits(cube[0], cube[1]))
    multiply_all(far)
    take(lambda cube, bridge: bits(cube[0], cube[2]))
    take(lambda cube, bridge: bits(cube[1], cube[2]))
    take(lambda cube, bridge: far | bits(cube[0]))
    multiply_all(*doubles)
    take(lambda cube, bridge: bits(*cube))
    take(lambda cube, bridge: far | bits(cube[1]))
    multiply_all(bits(*plan.cube))
    take(lambda cube, bridge: far | bits(cube[2]))
    multiply_all(*(far | node for node in singles))
    take(lambda cube, bridge: far | bits(cube[0], cube[1]))
    take(lambda cube, bridge: far | bits(cube[0], cube[2]))
    take(lambda cube, bridge: far | bits(cube[1], cube[2]))
    multiply_all(*(far | node for node in doubles))
    take(lambda cube, bridge: far | bits(*cube))
    multiply_all(far | bits(*plan.cube))

    def finish(ref, sem):
        pltpu.make_async_copy(ref, ref, sem).wait()

    finish(sky_buf.at[pl.ds(0, 9)], sky_send.at[0])
    finish(sky_buf.at[pl.ds(0, 8)], sky_send.at[1])
    finish(prod.at[pl.ds(0, 14)], prod_send)
    finish(prod.at[pl.ds(0, 2)], prod_own)
    finish(out_ref.at[pl.ds(0, WINDOWS // 8 * 7)], prod_recv)


def gather_kernel(
    coef_hbm, sky_hbm, hour_hbm, out_ref,
    coef_raw, sky_raw, hour_raw, coef_own, coef_sib, coef_next, coef_high, coef_low, sky_buf, relay, sky_high, sky_low, prod,
    load_sem, sky_sems, sky_send, coef_sems, coef_send, prod_send, prod_recv, prod_own,
):
    place = coordinates()
    h, s = device(place)
    me = h * 16 + s
    loads = [
        pltpu.make_async_copy(sky_hbm, sky_raw, load_sem.at[0]),
        pltpu.make_async_copy(hour_hbm.at[pl.ds(pl.multiple_of((me // 4) * 8, 8), 8)], hour_raw, load_sem.at[1]),
        pltpu.make_async_copy(coef_hbm, coef_raw, load_sem.at[2]),
    ]
    for load in loads:
        load.start()

    partners = [sibling(place)]
    for dimension in range(6):
        partners += [flipped(place, dimension), sibling(flipped(place, dimension))]
    barrier = pltpu.get_barrier_semaphore()
    for partner in partners:
        pl.semaphore_signal(barrier, inc=1, device_id=device(partner), device_id_type=MESH)

    loads[0].wait()
    loads[1].wait()
    sky_parts = two_parts(sky_raw[...])
    sky_buf[0, pl.ds(PATCHES - 1, 8), :] = jnp.zeros((8, 256), jnp.float32)
    for half in range(2):
        column = hour_raw[pl.ds((me % 4) * 2 + half, 1), :] - me * 256
        chosen = (lax.broadcasted_iota(jnp.int32, (256, 128), 0) == column).astype(jnp.bfloat16)
        ordered = sum(jnp.dot(part, chosen, preferred_element_type=jnp.float32) for part in sky_parts)
        sky_buf[0, pl.ds(0, PATCHES), pl.ds(half * 128, 128)] = ordered
    sky_high[pl.ds(576, 64), :] = jnp.zeros((64, 256), jnp.bfloat16)
    sky_low[pl.ds(576, 64), :] = jnp.zeros((64, 256), jnp.bfloat16)
    pl.semaphore_wait(barrier, len(partners))


    for core in range(2):
        @pl.when(place[3] == core)
        def _(core=core):
            exchange(
                (*place[:3], core), load_sem.at[2], out_ref, coef_raw, coef_own, coef_sib, coef_next, coef_high, coef_low,
                sky_buf, relay, sky_high, sky_low, prod, sky_sems, sky_send, coef_sems, coef_send, prod_send, prod_recv,
                prod_own, coef_hbm,
            )


def irradiance(coefficients, sky, hours):
    coefficients, sky, hours = [pltpu.with_memory_space_constraint(a, pltpu.HBM) for a in (coefficients, sky, hours)]
    f32, bf16 = jnp.float32, jnp.bfloat16
    vmem, dma = pltpu.VMEM, pltpu.SemaphoreType.DMA
    return pl.pallas_call(
        gather_kernel,
        out_shape=jax.ShapeDtypeStruct((WINDOWS, POINTS, WINDOW), f32),
        in_specs=[pl.BlockSpec(memory_space=pltpu.HBM)] * 3,
        out_specs=pl.BlockSpec(memory_space=pl.ANY),
        scratch_shapes=[
            vmem((PATCHES, 1, 512), f32),
            vmem((PATCHES, 256), f32),
            vmem((8, 128), jnp.int32),
            vmem((512, DEPTH), f32),
            vmem((3, 64, DEPTH), f32),
            vmem((3, 2, 64, DEPTH), f32),
            vmem((512, DEPTH), bf16),
            vmem((512, DEPTH), bf16),
            vmem((SLOTS, ROWS, 256), f32),
            vmem((6, 200, 256), f32),
            vmem((DEPTH, 256), bf16),
            vmem((DEPTH, 256), bf16),
            vmem((SLOTS, 2, 512, 128), f32),
            dma((3,)),
            dma((SLOTS + 6, 3)),
            dma((2,)),
            dma((7, 2)),
            dma((7,)),
            dma,
            dma,
            dma,
        ],
        compiler_params=pltpu.CompilerParams(
            collective_id=0, has_side_effects=True, vmem_limit_bytes=32 << 20
        ),
        name="irradiance",
    )(coefficients, sky, hours)


GROUP = 32
BUFFERS = 8


def thermal_kernel(flux_ref, air_ref, module_ref, out_hbm, means, buffers, sems):
    f32, bf16 = jnp.float32, jnp.bfloat16
    onehot = (lax.broadcasted_iota(jnp.int32, (MODS, POINTS), 0) == module_ref[...]).astype(bf16)
    both = jnp.concatenate([onehot, onehot], axis=1)
    none = jnp.zeros_like(both)
    pair = jnp.concatenate([jnp.concatenate([both, none], axis=1), jnp.concatenate([none, both], axis=1)], axis=0)
    row = lax.broadcasted_iota(jnp.int32, (WINDOW, WINDOW), 0)
    col = lax.broadcasted_iota(jnp.int32, (WINDOW, WINDOW), 1)
    summing = jnp.concatenate([(row <= col).astype(bf16), (row > col).astype(bf16)], axis=0)
    name = lax.broadcasted_iota(jnp.int32, (MODS, WINDOW), 0).astype(bf16)
    index = lax.dot_general(onehot, name, (((0,), (0,)), ((), ())), preferred_element_type=f32)
    index = index.astype(jnp.int32)
    means[pl.ds(0, MODS), :] = jnp.zeros((MODS, WINDOW), f32)

    def copy(group):
        slot = group % BUFFERS
        columns = pl.ds(group * GROUP * WINDOW, GROUP * WINDOW)
        return pltpu.make_async_copy(buffers.at[slot], out_hbm.at[:, columns], sems.at[slot])

    groups = WINDOWS // GROUP
    for group in range(groups):
        if group >= BUFFERS:
            copy(group - BUFFERS).wait()
        start = group * GROUP
        for w in range(start, start + GROUP, 2):
            parts = jnp.concatenate([*two_parts(flux_ref[w]), *two_parts(flux_ref[w + 1])], axis=0)
            mean = jnp.dot(pair, parts, preferred_element_type=f32) / (POINTS // MODS)
            means[pl.ds((w + 1) * MODS, 2 * MODS), :] = mean
        now = two_parts(means[pl.ds((start + 1) * MODS, GROUP * MODS), :])
        before = two_parts(means[pl.ds(start * MODS, GROUP * MODS), :])
        heat = jnp.zeros((GROUP * MODS, WINDOW), f32)
        for part in range(2):
            windows = jnp.concatenate([now[part], before[part]], axis=1)
            heat = heat + jnp.dot(windows, summing, preferred_element_type=f32)
        heat = heat / WINDOW
        for w in range(GROUP):
            warmth = air_ref[pl.ds(start + w, 1), :] + WARMUP * heat[w * MODS : (w + 1) * MODS, :]
            scale = 1.0 - LOSS * (warmth - NOMINAL)
            for r in range(POINTS // 8):
                rows = pl.ds(r * 8, 8)
                spread = jnp.take_along_axis(scale, index[r * 8 : (r + 1) * 8, :], axis=0)
                buffers[group % BUFFERS, rows, pl.ds(w * WINDOW, WINDOW)] = flux_ref[start + w, rows, :] * spread
        copy(group).start()
    for group in range(groups - BUFFERS, groups):
        copy(group).wait()


def thermal_power(flux, air, modules):
    return pl.pallas_call(
        thermal_kernel,
        out_shape=jax.ShapeDtypeStruct((POINTS, STEPS), jnp.float32),
        in_specs=[pl.BlockSpec(memory_space=pltpu.VMEM)] * 3,
        out_specs=pl.BlockSpec(memory_space=pl.ANY),
        scratch_shapes=[
            pltpu.VMEM(((WINDOWS + 1) * MODS, WINDOW), jnp.float32),
            pltpu.VMEM((BUFFERS, POINTS, GROUP * WINDOW), jnp.float32),
            pltpu.SemaphoreType.DMA((BUFFERS,)),
        ],
        compiler_params=pltpu.CompilerParams(vmem_limit_bytes=28 << 20),
        name="thermal",
    )(flux, air, modules)


def shards(coefficients, sky, outdoor_air_warmth, hour_column, module_of):
    flux = irradiance(coefficients, sky, hour_column.reshape(WINDOWS, WINDOW))
    power = thermal_power(flux, outdoor_air_warmth.reshape(WINDOWS, WINDOW), module_of.reshape(1, POINTS))
    return power.reshape(1, 1, POINTS, STEPS)


def solution(mesh):
    return jax.shard_map(
        shards,
        mesh=mesh,
        in_specs=(
            P(None, "sensor", None),
            P(None, ("hours", "sensor")),
            P(),
            P(),
            P("sensor", "hours", None),
        ),
        out_specs=P("sensor", "hours", None, None),
        check_vma=False,
    )
```
